32 devices in a mesh: cls: 8 (over z, x), rot: 4 (over y, core).
Axes of the slice: x: 2, y: 2, z: 4, core: 2. Of those that a mesh axis runs over, the one named last changes fastest.
Arguments:
- particles: bfloat16 [384, 64, 384], P('cls'), may hold values from -6 to 6
- references: bfloat16 [512, 64, 384], P('cls'), may hold values from -0.09 to 0.09
- noise_weights: float32 [64], replicated, may hold values from 0.1 to 1
- offsets: int32 [384], P('cls'), may hold values from 0 to 383
- sig_classes: int32 [384, 3], P('cls'), may hold values from 0 to 511, as said below
Outputs:
- log_evidence: float32 [384], P('cls')
- class_sums: float32 [512, 64, 384], P('cls', 'rot')
The draws below stay inside these ranges and needn't reach their ends.
Inputs may be any that keep to these rules, and one draw needn't show every extreme that they name: `sig_classes`: each particle lists 3 different classes. In each aligned block of 48 particles (those of one index of cls), at most 36 particles list a class of one owner (one value of id // 64); one owner, the same for all blocks, is listed by exactly 36 particles of every block.
All inputs are finite; a program needn't handle non-finite values.
Results may differ from the reference program's by a relative error of at most 0.0047.
Values may be sent and summed in bfloat16 or wider, within the bound.
A program may use at most 128 MiB of HBM per device.

```python
import math
import jax
import jax.numpy as jnp
from jax import lax

RADII = 64
ANGLES = 384
ROTS = 48
CLASSES = 512
K = 3
P_DEV = 48
PARTICLES = 384
CPD = 64
CAP = 36
ASTEP = 8


def draw_references(key, part):
    values = jax.random.normal(jax.random.fold_in(key, 11), (CLASSES, RADII, ANGLES), jnp.float32)
    return (jnp.clip(values, -6.0, 6.0) * 0.015).astype(jnp.bfloat16)


def draw_sig_classes(key, part):
    owner_count = CLASSES // CPD
    block_count = PARTICLES // P_DEV
    hottest = jax.random.randint(jax.random.fold_in(key, 7), (), 0, owner_count)

    def one_block(block_key):
        owner_pool = jnp.arange(owner_count * CAP, dtype=jnp.int32) // CAP
        priority = jax.random.permutation(jax.random.fold_in(block_key, 1), owner_count * CAP).astype(jnp.int32)
        priority = jnp.where(owner_pool == hottest, -1, priority)
        ordering = jnp.argsort(priority, stable=True)
        chosen = owner_pool[ordering][:K * P_DEV]
        owners = chosen.reshape(K, P_DEV).T
        shuffle = jax.random.permutation(jax.random.fold_in(block_key, 2), P_DEV)
        owners = owners[shuffle]
        offset_base = jax.random.randint(jax.random.fold_in(block_key, 3), (P_DEV, 1), 0, CPD)
        shifted = jax.random.randint(jax.random.fold_in(block_key, 4), (P_DEV, 1), 0, K)
        column = (jnp.arange(K, dtype=jnp.int32)[None, :] + shifted) % K
        owners = jnp.take_along_axis(owners, column, axis=1)
        inner_index = (offset_base + column) % CPD
        return owners * CPD + inner_index
    block_keys = jax.vmap(lambda block_index: jax.random.fold_in(key, 100 + block_index))(jnp.arange(block_count))
    return jax.vmap(one_block)(block_keys).reshape(PARTICLES, K).astype(jnp.int32)


def touch_ends(entries, key, smallest, high):
    longest = entries.shape.index(max(entries.shape))
    spots = []
    for shift in (0, 1):
        where = [jax.random.randint(jax.random.fold_in(key, axis), (), 0, length) for axis, length in enumerate(entries.shape)]
        where[longest] = (where[longest] + shift) % entries.shape[longest]
        spots.append(tuple(where))
    return entries.at[spots[0]].set(smallest).at[spots[1]].set(high)


def block_levels(own_key, extent, shards, smallest, largest):
    loudness = 1.0
    for axis_at, shards_of in shards:
        draws = jax.random.uniform(jax.random.fold_in(jax.random.fold_in(own_key, 6), axis_at), (shards_of,), jnp.float32, smallest / len(shards), largest / len(shards))
        loudness = loudness * jnp.repeat(jnp.exp(draws), extent[axis_at] // shards_of).reshape((-1,) + (1,) * (len(extent) - 1 - axis_at))
    return loudness


def normal_values(stream_key, dims, width, limit, cuts=(), kind=jnp.bfloat16):
    entries = width * jax.random.normal(stream_key, dims, jnp.float32)
    if cuts:
        entries = entries * block_levels(stream_key, dims, cuts, -0.22, 0.18)
    return jnp.clip(entries, -limit, limit).astype(kind)


def setup_inputs(seed: int = 0) -> dict:
    key_list = jax.random.split(jax.random.key(seed), 6)
    particles = normal_values(key_list[0], (PARTICLES, RADII, ANGLES), 1.0, 6.0, ((0, 8),))
    references = draw_references(jax.random.fold_in(key_list[5], 71), 0)
    noise_weights = jnp.clip(jnp.exp(jax.random.uniform(key_list[2], (RADII,), jnp.float32, math.log(0.1), math.log(1.0))), 0.1, 1.0)
    offsets = touch_ends(jax.random.randint(key_list[3], (PARTICLES,), 0, ANGLES), jax.random.fold_in(key_list[3], 1), 0, ANGLES - 1).astype(jnp.int32)
    sig_classes = draw_sig_classes(jax.random.fold_in(key_list[5], 71), 0)
    return dict(particles=particles, references=references, noise_weights=noise_weights, offsets=offsets, sig_classes=sig_classes)


def reference(particles, references, noise_weights, offsets, sig_classes):
    angle_iota = jnp.arange(ANGLES, dtype=jnp.int32)
    source_index = (angle_iota[None, :] + offsets[:, None]) % ANGLES
    aligned = jnp.take_along_axis(particles, source_index[:, None, :], axis=2)
    cycle_weights = noise_weights.astype(jnp.float32)[None, :, None]
    raw_images = references.astype(jnp.float32)
    weighted = (raw_images * cycle_weights).astype(jnp.bfloat16)
    energy = 0.5 * jnp.sum(cycle_weights * raw_images * raw_images, axis=(1, 2))
    shift_table = jnp.arange(ROTS, dtype=jnp.int32) * ASTEP
    forward = (angle_iota[None, :] - shift_table[:, None]) % ANGLES
    backward = (angle_iota[None, :] + shift_table[:, None]) % ANGLES

    def score_one(item):
        image, classes = item
        picked = weighted[classes]
        rotated = jnp.take(picked, forward, axis=2)
        corr = jnp.einsum("ra,krta->kt", image.astype(jnp.float32), rotated.astype(jnp.float32))
        return corr - energy[classes][:, None]

    scores = lax.map(score_one, (aligned, sig_classes))
    exponentials = jnp.exp(scores)
    totals = jnp.sum(exponentials, axis=(1, 2))
    log_evidence = jnp.log(totals)
    posterior = (exponentials * (1.0 / totals)[:, None, None]).astype(jnp.bfloat16)

    def add_one(running, item):
        image, classes, weight_rows = item
        shifted = jnp.take(image, backward, axis=1)
        contrib = jnp.einsum("kt,rta->kra", weight_rows.astype(jnp.float32), shifted.astype(jnp.float32))
        return running.at[classes].add(contrib), None

    start_sums = jnp.zeros((CLASSES, RADII, ANGLES), jnp.float32)
    class_sums = lax.scan(add_one, start_sums, (aligned, sig_classes, posterior))[0]
    return log_evidence, class_sums
```

```python
import functools

import jax
import jax.numpy as jnp
from jax import lax
from jax.experimental import pallas as pl
from jax.experimental.pallas import tpu as pltpu
from jax.sharding import PartitionSpec as P

ROTS = 48
GROUP = 8
LANES = 128
SPAN = LANES // GROUP
BATCH = 8
F32 = jnp.float32
BF16 = jnp.bfloat16


def swap_blocks(pages):
    block = lax.broadcasted_iota(jnp.int32, pages[0].shape, 1) // SPAN
    for step in (1, 2, 4):
        high = (block & step) != 0
        changed = list(pages)
        for low_index in range(GROUP):
            if low_index & step:
                continue
            low_page, high_page = pages[low_index], pages[low_index | step]
            changed[low_index] = jnp.where(high, pltpu.roll(high_page, SPAN * step, 1), low_page)
            changed[low_index | step] = jnp.where(
                high, high_page, pltpu.roll(low_page, LANES - SPAN * step, 1)
            )
        pages = changed
    return pages


def split_angles(rows, flipped):
    flipped[...] = rows.T
    return swap_blocks([flipped[pl.ds(s, ROTS, stride=GROUP), :] for s in range(GROUP)])


def particle_kernel(rot_ref, offset_ref, image_ref, page_ref, rows, flipped):
    first = pl.program_id(0) * GROUP
    cycles, angles = image_ref.shape[1:]
    if cycles < SPAN:
        rows[...] = jnp.zeros_like(rows)
    for member in range(GROUP):
        shift = lax.rem(angles - offset_ref[first + member], angles)
        rows[pl.ds(member * SPAN, cycles), :] = pltpu.roll(
            image_ref[member].astype(F32), shift, 1
        )
    pages = split_angles(rows[...], flipped)
    for member in range(GROUP):
        page_ref[member] = pages[member].astype(BF16)


def reference_kernel(rot_ref, image_ref, weight_ref, page_ref, energy_ref, flipped):
    cycles, angles = image_ref.shape[1:]
    images = image_ref[...].astype(F32)
    weights = weight_ref[...][None]
    weighted = (images * weights).astype(BF16).astype(F32)
    energy = jnp.sum(jnp.sum(weights * images * images, axis=2), axis=1, keepdims=True)
    energy_ref[...] = jnp.broadcast_to(0.5 * energy, energy_ref.shape)
    if cycles < SPAN:
        spare = jnp.zeros((GROUP, SPAN - cycles, angles), F32)
        weighted = jnp.concatenate([weighted, spare], axis=1)
    pages = split_angles(weighted.reshape(LANES, angles), flipped)
    source = lax.broadcasted_iota(jnp.int32, (ROTS, LANES), 0)
    target = lax.broadcasted_iota(jnp.int32, (ROTS, LANES), 1)
    reverse = jnp.where(lax.rem(source + target, ROTS) == 0, 1.0, 0.0).astype(BF16)
    for member in range(GROUP):
        page_ref[member] = lax.dot_general(
            pages[member].astype(BF16), reverse, (((0,), (0,)), ((), ())), preferred_element_type=F32
        ).astype(BF16)


def score_kernel(count_ref, list_ref, image_ref, class_ref, energy_ref, out_ref, held):
    held[...] = jnp.zeros_like(held)
    half = out_ref.shape[0]

    def batch(step, carry):
        products = []
        for member in range(BATCH):
            at = step * BATCH + member
            image = image_ref[list_ref[1, at]]
            products.append(
                jnp.dot(image, class_ref[list_ref[2, at]], preferred_element_type=F32)
            )
        for member in range(BATCH):
            at = step * BATCH + member
            skewed = pltpu.roll(products[member], 0, 1, stride=1, stride_axis=0)
            score = jnp.sum(skewed, axis=0, keepdims=True)
            held[pl.ds(list_ref[0, at], 1), :] = score - energy_ref[pl.ds(list_ref[2, at], 1), :]
        return carry

    lax.fori_loop(0, count_ref[0], batch, 0)
    lane = lax.broadcasted_iota(jnp.int32, (half, LANES), 1)
    low = pltpu.roll(held[pl.ds(0, half), :], LANES - ROTS, 1)
    high = pltpu.roll(held[pl.ds(half, half), :], LANES // 2 - ROTS, 1)
    inside = (lane % (LANES // 2)) < ROTS
    out_ref[...] = jnp.where(inside, jnp.where(lane < LANES // 2, low, high), 0.0)


def sum_kernel(
    count_ref, list_ref, score_ref, image_ref, out_ref, total_ref, weight, sums, flipped
):
    half = score_ref.shape[0]
    particles = total_ref.shape[0]
    class_local, cycles, angles = out_ref.shape
    lane = lax.broadcasted_iota(jnp.int32, (half, LANES), 1)
    inside = (lane % (LANES // 2)) < ROTS
    grown = jnp.where(inside, jnp.exp(score_ref[...]), 0.0)
    lows = jnp.where(lane < LANES // 2, grown, 0.0)
    highs = pltpu.roll(grown - lows, LANES // 2, 1)
    weight[pl.ds(0, half), :] = lows
    weight[pl.ds(half, half), :] = highs
    listed = 2 * half // particles
    total = jnp.zeros((particles, 1), F32)
    for k in range(listed):
        total += jnp.sum(weight[pl.ds(k * particles, particles), :], axis=1, keepdims=True)
    total_ref[...] = jnp.broadcast_to(total, total_ref.shape)
    inverse = 1.0 / total
    for k in range(listed):
        rows = pl.ds(k * particles, particles)
        posterior = weight[rows, :] * inverse
        weight[rows, :] = posterior + pltpu.roll(posterior, LANES - ROTS, 1)
    weight[pl.ds(2 * half, GROUP), :] = jnp.zeros((GROUP, LANES), F32)
    sums[...] = jnp.zeros_like(sums)

    def batch(step, carry):
        products = []
        for member in range(BATCH):
            at = step * BATCH + member
            row = weight[pl.ds(list_ref[0, at], 1), :]
            skewed = pltpu.roll(
                jnp.broadcast_to(row, (ROTS, LANES)), 0, 1, stride=1, stride_axis=0
            )
            image = image_ref[list_ref[1, at]]
            products.append(
                jnp.dot(skewed.astype(BF16)[:, :ROTS], image, preferred_element_type=F32)
            )
        for member in range(BATCH):
            own = list_ref[2, step * BATCH + member]
            sums[own] = sums[own] + products[member]
        return carry

    lax.fori_loop(0, count_ref[0], batch, 0)

    def write(group, carry):
        first = group * GROUP
        pages = swap_blocks([sums[first + member] for member in range(GROUP)])
        for s in range(GROUP):
            flipped[pl.ds(s, ROTS, stride=GROUP), :] = pages[s]
        out_ref[pl.ds(first, GROUP)] = flipped[...].T.reshape(GROUP, SPAN, angles)[:, :cycles]
        return carry

    lax.fori_loop(0, class_local // GROUP, write, 0)


VMEM = pl.BlockSpec(memory_space=pltpu.VMEM)
SMEM = pl.BlockSpec(memory_space=pltpu.SMEM)


def shards(particles, references, noise_weights, offsets, sig_classes):
    owner_count = lax.axis_size("cls")
    split_count = lax.axis_size("rot")
    home_count, cycle_count, angle_count = particles.shape
    class_local = references.shape[0]
    list_length = sig_classes.shape[1]
    particle_count = home_count * owner_count
    cycles = cycle_count // split_count
    pair_count = particle_count * list_length
    half = pair_count // 2
    me = lax.axis_index("cls")
    rot = lax.axis_index("rot").astype(jnp.int32)
    rot_arg = rot.reshape(1)
    limit = pltpu.CompilerParams(vmem_limit_bytes=56 << 20)

    classes = lax.all_gather(sig_classes, "cls", axis=0, tiled=True)
    classes = classes.T.reshape(pair_count)
    pair_iota = jnp.arange(pair_count, dtype=jnp.int32)
    mine = (classes // class_local) == me
    before = pair_iota[None, :] < pair_iota[:, None]
    place = jnp.sum(jnp.where(before & mine[None, :], 1, 0), axis=1)
    count = jnp.sum(mine.astype(jnp.int32))
    slots = jnp.arange(pair_count + BATCH, dtype=jnp.int32)
    hit = (place[None, :] == slots[:, None]) & mine[None, :]
    pick = lambda values: jnp.sum(jnp.where(hit, values[None, :], 0), axis=1)
    unused = jnp.where(slots < count, 0, pair_count)
    work = jnp.stack(
        [
            pick(pair_iota) + unused,
            pick(pair_iota % particle_count),
            pick(classes % class_local),
        ]
    )
    batches = ((count + BATCH - 1) // BATCH).reshape(1)

    image_block = (GROUP, cycles, angle_count)
    pages = pl.pallas_call(
        particle_kernel,
        out_shape=jax.ShapeDtypeStruct((home_count, ROTS, LANES), BF16),
        grid_spec=pltpu.PrefetchScalarGridSpec(
            num_scalar_prefetch=2,
            grid=(home_count // GROUP,),
            in_specs=[pl.BlockSpec(image_block, lambda g, r, o: (g, r[0], 0))],
            out_specs=pl.BlockSpec((GROUP, ROTS, LANES), lambda g, r, o: (g, 0, 0)),
            scratch_shapes=[
                pltpu.VMEM((LANES, angle_count), F32),
                pltpu.VMEM((angle_count, LANES), F32),
            ],
        ),
        name="align_particles",
    )(rot_arg, offsets, particles)
    gathered = lax.all_gather(pages, "cls", axis=0, tiled=True)

    own_weights = lax.dynamic_slice_in_dim(noise_weights, rot * cycles, cycles).reshape(cycles, 1)
    class_pages, energy = pl.pallas_call(
        reference_kernel,
        out_shape=(
            jax.ShapeDtypeStruct((class_local, LANES, LANES), BF16),
            jax.ShapeDtypeStruct((class_local, LANES), F32),
        ),
        grid_spec=pltpu.PrefetchScalarGridSpec(
            num_scalar_prefetch=1,
            grid=(class_local // GROUP,),
            in_specs=[
                pl.BlockSpec(image_block, lambda g, r: (g, r[0], 0)),
                pl.BlockSpec((cycles, 1), lambda g, r: (0, 0)),
            ],
            out_specs=(
                pl.BlockSpec((GROUP, LANES, LANES), lambda g, r: (g, 0, 0)),
                pl.BlockSpec((GROUP, LANES), lambda g, r: (g, 0)),
            ),
            scratch_shapes=[pltpu.VMEM((angle_count, LANES), F32)],
        ),
        name="weight_references",
    )(rot_arg, references, own_weights)

    scores = pl.pallas_call(
        score_kernel,
        out_shape=jax.ShapeDtypeStruct((half, LANES), F32),
        in_specs=[SMEM, SMEM, VMEM, VMEM, VMEM],
        out_specs=VMEM,
        scratch_shapes=[pltpu.VMEM((pair_count + GROUP, LANES), F32)],
        compiler_params=limit,
        name="score_pairs",
    )(batches, work, gathered, class_pages, energy)
    scores = lax.psum(scores, ("cls", "rot"))

    class_sums, total = pl.pallas_call(
        sum_kernel,
        out_shape=(
            jax.ShapeDtypeStruct((class_local, cycles, angle_count), F32),
            jax.ShapeDtypeStruct((particle_count, LANES), F32),
        ),
        in_specs=[SMEM, SMEM, VMEM, VMEM],
        out_specs=(VMEM, VMEM),
        scratch_shapes=[
            pltpu.VMEM((pair_count + GROUP, LANES), F32),
            pltpu.VMEM((class_local, ROTS, LANES), F32),
            pltpu.VMEM((angle_count, LANES), F32),
        ],
        compiler_params=limit,
        name="sum_classes",
    )(batches, work, scores, gathered)
    own_total = lax.dynamic_slice_in_dim(total, me * home_count, home_count)[:, 0]
    return (jnp.log(own_total), class_sums)


def solution(mesh):
    in_specs = (P("cls", None, None), P("cls", None, None), P(), P("cls"), P("cls", None))
    out_specs = (P("cls"), P("cls", "rot", None))
    return jax.shard_map(shards, mesh=mesh, in_specs=in_specs, out_specs=out_specs, check_vma=False)
```

```python
import functools

import jax
import jax.numpy as jnp
from jax import lax
from jax.experimental import pallas as pl
from jax.experimental.pallas import tpu as pltpu
from jax.sharding import PartitionSpec as P

ROTS = 48
GROUP = 8
LANES = 128
SPAN = LANES // GROUP
BATCH = 8
UNLISTED = -1e30
F32 = jnp.float32
BF16 = jnp.bfloat16


def swap_blocks(pages):
    block = lax.broadcasted_iota(jnp.int32, pages[0].shape, 1) // SPAN
    for step in (1, 2, 4):
        high = (block & step) != 0
        changed = list(pages)
        for low_index in range(GROUP):
            if low_index & step:
                continue
            low_page, high_page = pages[low_index], pages[low_index | step]
            changed[low_index] = jnp.where(high, pltpu.roll(high_page, SPAN * step, 1), low_page)
            changed[low_index | step] = jnp.where(
                high, high_page, pltpu.roll(low_page, LANES - SPAN * step, 1)
            )
        pages = changed
    return pages


def split_angles(rows, flipped):
    flipped[...] = rows.T
    return swap_blocks([flipped[pl.ds(s, ROTS, stride=GROUP), :] for s in range(GROUP)])


def particle_kernel(rot_ref, offset_ref, image_ref, page_ref, rows, flipped):
    first = pl.program_id(0) * GROUP
    cycles, angles = image_ref.shape[1:]
    if cycles < SPAN:
        rows[...] = jnp.zeros_like(rows)
    for member in range(GROUP):
        shift = lax.rem(angles - offset_ref[first + member], angles)
        rows[pl.ds(member * SPAN, cycles), :] = pltpu.roll(
            image_ref[member].astype(F32), shift, 1
        )
    pages = split_angles(rows[...], flipped)
    for member in range(GROUP):
        page_ref[member] = pages[member].astype(BF16)


def reference_kernel(rot_ref, image_ref, weight_ref, page_ref, energy_ref, flipped):
    cycles, angles = image_ref.shape[1:]
    images = image_ref[...].astype(F32)
    weights = weight_ref[...][None]
    weighted = (images * weights).astype(BF16).astype(F32)
    energy = jnp.sum(jnp.sum(weights * images * images, axis=2), axis=1, keepdims=True)
    energy_ref[...] = jnp.broadcast_to(0.5 * energy, energy_ref.shape)
    if cycles < SPAN:
        spare = jnp.zeros((GROUP, SPAN - cycles, angles), F32)
        weighted = jnp.concatenate([weighted, spare], axis=1)
    pages = split_angles(weighted.reshape(LANES, angles), flipped)
    source = lax.broadcasted_iota(jnp.int32, (ROTS, LANES), 0)
    target = lax.broadcasted_iota(jnp.int32, (ROTS, LANES), 1)
    reverse = jnp.where(lax.rem(source + target, ROTS) == 0, 1.0, 0.0).astype(BF16)
    for member in range(GROUP):
        page_ref[member] = lax.dot_general(
            pages[member].astype(BF16), reverse, (((0,), (0,)), ((), ())), preferred_element_type=F32
        ).astype(BF16)


def score_kernel(count_ref, list_ref, image_ref, class_ref, energy_ref, out_ref, held):
    held[...] = jnp.full_like(held, UNLISTED)
    half = out_ref.shape[0]

    def batch(step, carry):
        products = []
        for member in range(BATCH):
            at = step * BATCH + member
            image = image_ref[list_ref[1, at]]
            products.append(
                jnp.dot(image, class_ref[list_ref[2, at]], preferred_element_type=F32)
            )
        for member in range(BATCH):
            at = step * BATCH + member
            skewed = pltpu.roll(products[member], 0, 1, stride=1, stride_axis=0)
            score = jnp.sum(skewed, axis=0, keepdims=True)
            held[pl.ds(list_ref[0, at], 1), :] = score - energy_ref[pl.ds(list_ref[2, at], 1), :]
        return carry

    lax.fori_loop(0, count_ref[0], batch, 0)
    lane = lax.broadcasted_iota(jnp.int32, (half, LANES), 1)
    low = pltpu.roll(held[pl.ds(0, half), :], LANES - ROTS, 1)
    high = pltpu.roll(held[pl.ds(half, half), :], LANES // 2 - ROTS, 1)
    inside = (lane % (LANES // 2)) < ROTS
    out_ref[...] = jnp.where(inside, jnp.where(lane < LANES // 2, low, high), UNLISTED)


def push(peers, source, inbox, sends, arrivals):
    copies = [
        pltpu.make_async_remote_copy(
            src_ref=source(peer),
            dst_ref=inbox.at[slot],
            send_sem=sends.at[slot],
            recv_sem=arrivals.at[slot],
            device_id=peer,
            device_id_type=pl.DeviceIdType.MESH,
        )
        for slot, peer in enumerate(peers)
    ]
    for copy in copies:
        copy.start()
    return copies


def peers_along(axis):
    size = lax.axis_size(axis)
    own = lax.axis_index(axis)
    return [{axis: lax.rem(own + step, size)} for step in range(1, size)]


def greet(peers):
    barrier = pltpu.get_barrier_semaphore()
    for peer in peers:
        pl.semaphore_signal(barrier, inc=1, device_id=peer, device_id_type=pl.DeviceIdType.MESH)
    pl.semaphore_wait(barrier, len(peers))


def list_kernel(own_ref, out_ref, inbox, sends, arrivals):
    peers = peers_along("cls")
    size = len(peers) + 1
    me = lax.axis_index("cls")
    greet(peers)
    copies = push(peers, lambda peer: own_ref, inbox, sends, arrivals)
    out_ref[me] = own_ref[...]
    for slot, copy in enumerate(copies):
        copy.wait_recv()
        out_ref[lax.rem(me + size - slot - 1, size)] = inbox[slot]
    for copy in copies:
        copy.wait_send()


def reduce_kernel(
    score_ref, out_ref, pair_ref, parts, share, spread, tally, tallies, summed, wide,
    send_a, send_b, send_c, send_d, recv_a, recv_b, recv_c, recv_d,
):
    rots, owners = peers_along("rot"), peers_along("cls")
    splits = len(rots) + 1
    rot = lax.axis_index("rot")
    rows = share.shape[0]
    greet(rots + owners)

    def part(index):
        return pl.ds(pl.multiple_of(index * rows, GROUP), rows)

    first = push(rots, lambda peer: score_ref.at[part(peer["rot"])], parts, send_a, recv_a)
    total = score_ref[part(rot), :]
    for slot, copy in enumerate(first):
        copy.wait_recv()
        total = total + parts[slot]
    share[...] = total
    second = push(rots, lambda peer: share, spread, send_b, recv_b)
    grown = jnp.concatenate(
        [jnp.exp(total), jnp.zeros((tally.shape[1] - rows, LANES), F32)], axis=0
    ).T
    tally[...] = jnp.zeros_like(tally)
    tally[pl.ds(0, 1), :] = jnp.sum(grown[: LANES // 2], axis=0, keepdims=True)
    tally[pl.ds(1, 1), :] = jnp.sum(grown[LANES // 2 :], axis=0, keepdims=True)
    third = push(owners, lambda peer: tally, tallies, send_c, recv_c)
    out_ref[part(rot), :] = total
    sums = tally[...]
    for slot, copy in enumerate(third):
        copy.wait_recv()
        sums = sums + tallies[slot]
    summed[...] = sums
    fourth = push(rots, lambda peer: summed, wide, send_d, recv_d)
    pair_ref[rot] = sums
    for slot in range(len(rots)):
        source = lax.rem(rot + splits - slot - 1, splits)
        second[slot].wait_recv()
        out_ref[part(source), :] = spread[slot]
        fourth[slot].wait_recv()
        pair_ref[source] = wide[slot]
    for copy in first + second + third + fourth:
        copy.wait_send()


def sum_kernel(
    count_ref, list_ref, score_ref, total_ref, image_ref, out_ref, weight, sums, flipped
):
    half = score_ref.shape[0]
    particles = total_ref.shape[0]
    class_local, cycles, angles = out_ref.shape
    lane = lax.broadcasted_iota(jnp.int32, (half, LANES), 1)
    grown = jnp.exp(score_ref[...])
    lows = jnp.where(lane < LANES // 2, grown, 0.0)
    weight[pl.ds(0, half), :] = lows
    weight[pl.ds(half, half), :] = pltpu.roll(grown - lows, LANES // 2, 1)
    inverse = 1.0 / total_ref[...]
    for k in range(2 * half // particles):
        rows = pl.ds(k * particles, particles)
        posterior = weight[rows, :] * inverse
        weight[rows, :] = posterior + pltpu.roll(posterior, LANES - ROTS, 1)
    weight[pl.ds(2 * half, GROUP), :] = jnp.zeros((GROUP, LANES), F32)
    sums[...] = jnp.zeros_like(sums)

    def batch(step, carry):
        products = []
        for member in range(BATCH):
            at = step * BATCH + member
            row = weight[pl.ds(list_ref[0, at], 1), :]
            skewed = pltpu.roll(
                jnp.broadcast_to(row, (ROTS, LANES)), 0, 1, stride=1, stride_axis=0
            )
            image = image_ref[list_ref[1, at]]
            products.append(
                jnp.dot(skewed.astype(BF16)[:, :ROTS], image, preferred_element_type=F32)
            )
        for member in range(BATCH):
            own = list_ref[2, step * BATCH + member]
            sums[own] = sums[own] + products[member]
        return carry

    lax.fori_loop(0, count_ref[0], batch, 0)

    def write(group, carry):
        first = group * GROUP
        pages = swap_blocks([sums[first + member] for member in range(GROUP)])
        for s in range(GROUP):
            flipped[pl.ds(s, ROTS, stride=GROUP), :] = pages[s]
        out_ref[pl.ds(first, GROUP)] = flipped[...].T.reshape(GROUP, SPAN, angles)[:, :cycles]
        return carry

    lax.fori_loop(0, class_local // GROUP, write, 0)


VMEM = pl.BlockSpec(memory_space=pltpu.VMEM)
SMEM = pl.BlockSpec(memory_space=pltpu.SMEM)


def shards(particles, references, noise_weights, offsets, sig_classes):
    owner_count = lax.axis_size("cls")
    split_count = lax.axis_size("rot")
    home_count, cycle_count, angle_count = particles.shape
    class_local = references.shape[0]
    list_length = sig_classes.shape[1]
    particle_count = home_count * owner_count
    cycles = cycle_count // split_count
    pair_count = particle_count * list_length
    half = pair_count // 2
    me = lax.axis_index("cls")
    rot = lax.axis_index("rot").astype(jnp.int32)
    rot_arg = rot.reshape(1)
    limit = pltpu.CompilerParams(vmem_limit_bytes=56 << 20)

    owners, rots = owner_count - 1, split_count - 1
    own_list = jnp.pad(
        sig_classes.T, ((0, GROUP - list_length), (0, LANES - home_count)), constant_values=0
    )
    classes = pl.pallas_call(
        list_kernel,
        out_shape=jax.ShapeDtypeStruct((owner_count, GROUP, LANES), jnp.int32),
        in_specs=[VMEM],
        out_specs=VMEM,
        scratch_shapes=[pltpu.VMEM((owners, GROUP, LANES), jnp.int32)]
        + [pltpu.SemaphoreType.DMA((owners,))] * 2,
        compiler_params=pltpu.CompilerParams(collective_id=1, has_side_effects=True),
        name="exchange_lists",
    )(own_list)
    classes = classes[:, :list_length, :home_count].transpose(1, 0, 2).reshape(pair_count)
    pair_iota = jnp.arange(pair_count, dtype=jnp.int32)
    mine = (classes // class_local) == me
    before = pair_iota[None, :] < pair_iota[:, None]
    place = jnp.sum(jnp.where(before & mine[None, :], 1, 0), axis=1)
    count = jnp.sum(mine.astype(jnp.int32))
    slots = jnp.arange(pair_count + BATCH, dtype=jnp.int32)
    hit = (place[None, :] == slots[:, None]) & mine[None, :]
    pick = lambda values: jnp.sum(jnp.where(hit, values[None, :], 0), axis=1)
    unused = jnp.where(slots < count, 0, pair_count)
    work = jnp.stack(
        [
            pick(pair_iota) + unused,
            pick(pair_iota % particle_count),
            pick(classes % class_local),
        ]
    )
    batches = ((count + BATCH - 1) // BATCH).reshape(1)

    image_block = (GROUP, cycles, angle_count)
    pages = pl.pallas_call(
        particle_kernel,
        out_shape=jax.ShapeDtypeStruct((home_count, ROTS, LANES), BF16),
        grid_spec=pltpu.PrefetchScalarGridSpec(
            num_scalar_prefetch=2,
            grid=(home_count // GROUP,),
            in_specs=[pl.BlockSpec(image_block, lambda g, r, o: (g, r[0], 0))],
            out_specs=pl.BlockSpec((GROUP, ROTS, LANES), lambda g, r, o: (g, 0, 0)),
            scratch_shapes=[
                pltpu.VMEM((LANES, angle_count), F32),
                pltpu.VMEM((angle_count, LANES), F32),
            ],
        ),
        name="align_particles",
    )(rot_arg, offsets, particles)
    gathered = lax.all_gather(pages, "cls", axis=0, tiled=True)

    own_weights = lax.dynamic_slice_in_dim(noise_weights, rot * cycles, cycles).reshape(cycles, 1)
    class_pages, energy = pl.pallas_call(
        reference_kernel,
        out_shape=(
            jax.ShapeDtypeStruct((class_local, LANES, LANES), BF16),
            jax.ShapeDtypeStruct((class_local, LANES), F32),
        ),
        grid_spec=pltpu.PrefetchScalarGridSpec(
            num_scalar_prefetch=1,
            grid=(class_local // GROUP,),
            in_specs=[
                pl.BlockSpec(image_block, lambda g, r: (g, r[0], 0)),
                pl.BlockSpec((cycles, 1), lambda g, r: (0, 0)),
            ],
            out_specs=(
                pl.BlockSpec((GROUP, LANES, LANES), lambda g, r: (g, 0, 0)),
                pl.BlockSpec((GROUP, LANES), lambda g, r: (g, 0)),
            ),
            scratch_shapes=[pltpu.VMEM((angle_count, LANES), F32)],
        ),
        name="weight_references",
    )(rot_arg, references, own_weights)

    scores = pl.pallas_call(
        score_kernel,
        out_shape=jax.ShapeDtypeStruct((half, LANES), F32),
        in_specs=[SMEM, SMEM, VMEM, VMEM, VMEM],
        out_specs=VMEM,
        scratch_shapes=[pltpu.VMEM((pair_count + GROUP, LANES), F32)],
        compiler_params=limit,
        name="score_pairs",
    )(batches, work, gathered, class_pages, energy)
    share = half // split_count
    wide = -(-share // LANES) * LANES
    tile = pltpu.VMEM((GROUP, wide), F32)
    scores, pair_sums = pl.pallas_call(
        reduce_kernel,
        out_shape=(
            jax.ShapeDtypeStruct((half, LANES), F32),
            jax.ShapeDtypeStruct((split_count, GROUP, wide), F32),
        ),
        in_specs=[VMEM],
        out_specs=(VMEM, VMEM),
        scratch_shapes=[
            pltpu.VMEM((rots, share, LANES), F32),
            pltpu.VMEM((share, LANES), F32),
            pltpu.VMEM((rots, share, LANES), F32),
            tile,
            pltpu.VMEM((owners, GROUP, wide), F32),
            tile,
            pltpu.VMEM((rots, GROUP, wide), F32),
        ]
        + [pltpu.SemaphoreType.DMA((count_of,)) for count_of in (rots, rots, owners, rots)] * 2,
        compiler_params=pltpu.CompilerParams(
            collective_id=2, has_side_effects=True, vmem_limit_bytes=56 << 20
        ),
        name="exchange_scores",
    )(scores)
    pair_sums = pair_sums[:, :2, :share].transpose(1, 0, 2).reshape(list_length, particle_count)
    total = jnp.sum(pair_sums, axis=0)

    class_sums = pl.pallas_call(
        sum_kernel,
        out_shape=jax.ShapeDtypeStruct((class_local, cycles, angle_count), F32),
        in_specs=[SMEM, SMEM, VMEM, VMEM, VMEM],
        out_specs=VMEM,
        scratch_shapes=[
            pltpu.VMEM((pair_count + GROUP, LANES), F32),
            pltpu.VMEM((class_local, ROTS, LANES), F32),
            pltpu.VMEM((angle_count, LANES), F32),
        ],
        compiler_params=limit,
        name="sum_classes",
    )(batches, work, scores, total.reshape(particle_count, 1), gathered)
    own_total = lax.dynamic_slice_in_dim(total, me * home_count, home_count)
    return (jnp.log(own_total), class_sums)


def solution(mesh):
    in_specs = (P("cls", None, None), P("cls", None, None), P(), P("cls"), P("cls", None))
    out_specs = (P("cls"), P("cls", "rot", None))
    return jax.shard_map(shards, mesh=mesh, in_specs=in_specs, out_specs=out_specs, check_vma=False)
```

```python
import functools

import jax
import jax.numpy as jnp
from jax import lax
from jax.experimental import pallas as pl
from jax.experimental.pallas import tpu as pltpu
from jax.sharding import PartitionSpec as P

ROTS = 48
GROUP = 8
LANES = 128
SPAN = LANES // GROUP
BATCH = 8
UNLISTED = -1e30
F32 = jnp.float32
BF16 = jnp.bfloat16


def swap_blocks(pages):
    block = lax.broadcasted_iota(jnp.int32, pages[0].shape, 1) // SPAN
    for step in (1, 2, 4):
        high = (block & step) != 0
        changed = list(pages)
        for low_index in range(GROUP):
            if low_index & step:
                continue
            low_page, high_page = pages[low_index], pages[low_index | step]
            changed[low_index] = jnp.where(high, pltpu.roll(high_page, SPAN * step, 1), low_page)
            changed[low_index | step] = jnp.where(
                high, high_page, pltpu.roll(low_page, LANES - SPAN * step, 1)
            )
        pages = changed
    return pages


def split_angles(rows, flipped):
    flipped[...] = rows.T
    return swap_blocks([flipped[pl.ds(s, ROTS, stride=GROUP), :] for s in range(GROUP)])


def particle_kernel(rot_ref, offset_ref, image_ref, page_ref, rows, flipped):
    first = pl.program_id(0) * GROUP
    cycles, angles = image_ref.shape[1:]
    if cycles < SPAN:
        rows[...] = jnp.zeros_like(rows)
    for member in range(GROUP):
        shift = lax.rem(angles - offset_ref[first + member], angles)
        rows[pl.ds(member * SPAN, cycles), :] = pltpu.roll(
            image_ref[member].astype(F32), shift, 1
        )
    pages = split_angles(rows[...], flipped)
    for member in range(GROUP):
        page_ref[member] = pages[member].astype(BF16)


def reference_kernel(rot_ref, image_ref, weight_ref, page_ref, energy_ref, flipped):
    cycles, angles = image_ref.shape[1:]
    images = image_ref[...].astype(F32)
    weights = weight_ref[...][None]
    weighted = (images * weights).astype(BF16).astype(F32)
    energy = jnp.sum(jnp.sum(weights * images * images, axis=2), axis=1, keepdims=True)
    energy_ref[...] = jnp.broadcast_to(0.5 * energy, energy_ref.shape)
    if cycles < SPAN:
        spare = jnp.zeros((GROUP, SPAN - cycles, angles), F32)
        weighted = jnp.concatenate([weighted, spare], axis=1)
    pages = split_angles(weighted.reshape(LANES, angles), flipped)
    source = lax.broadcasted_iota(jnp.int32, (ROTS, LANES), 0)
    target = lax.broadcasted_iota(jnp.int32, (ROTS, LANES), 1)
    reverse = jnp.where(lax.rem(source + target, ROTS) == 0, 1.0, 0.0).astype(BF16)
    for member in range(GROUP):
        page_ref[member] = lax.dot_general(
            pages[member].astype(BF16), reverse, (((0,), (0,)), ((), ())), preferred_element_type=F32
        ).astype(BF16)


def score_kernel(count_ref, list_ref, image_ref, class_ref, energy_ref, out_ref, held):
    held[...] = jnp.full_like(held, UNLISTED)
    half = out_ref.shape[0]

    def batch(step, carry):
        products = []
        for member in range(BATCH):
            at = step * BATCH + member
            image = image_ref[list_ref[1, at]]
            products.append(
                jnp.dot(image, class_ref[list_ref[2, at]], preferred_element_type=F32)
            )
        for member in range(BATCH):
            at = step * BATCH + member
            skewed = pltpu.roll(products[member], 0, 1, stride=1, stride_axis=0)
            score = jnp.sum(skewed, axis=0, keepdims=True)
            held[pl.ds(list_ref[0, at], 1), :] = score - energy_ref[pl.ds(list_ref[2, at], 1), :]
        return carry

    lax.fori_loop(0, count_ref[0], batch, 0)
    lane = lax.broadcasted_iota(jnp.int32, (half, LANES), 1)
    low = pltpu.roll(held[pl.ds(0, half), :], LANES - ROTS, 1)
    high = pltpu.roll(held[pl.ds(half, half), :], LANES // 2 - ROTS, 1)
    inside = (lane % (LANES // 2)) < ROTS
    out_ref[...] = jnp.where(inside, jnp.where(lane < LANES // 2, low, high), UNLISTED)


def push(peers, source, inbox, sends, arrivals):
    copies = [
        pltpu.make_async_remote_copy(
            src_ref=source(peer),
            dst_ref=inbox.at[slot],
            send_sem=sends.at[slot],
            recv_sem=arrivals.at[slot],
            device_id=peer,
            device_id_type=pl.DeviceIdType.MESH,
        )
        for slot, peer in enumerate(peers)
    ]
    for copy in copies:
        copy.start()
    return copies


def peers_along(axis):
    size = lax.axis_size(axis)
    own = lax.axis_index(axis)
    return [{axis: lax.rem(own + step, size)} for step in range(1, size)]


def greet(peers):
    barrier = pltpu.get_barrier_semaphore()
    for peer in peers:
        pl.semaphore_signal(barrier, inc=1, device_id=peer, device_id_type=pl.DeviceIdType.MESH)
    pl.semaphore_wait(barrier, len(peers))


def gather_kernel(
    page_ref, own_ref, out_ref, list_ref, inbox, local_sem, list_sends, list_arrivals, sends, arrivals
):
    peers = peers_along("cls")
    size = len(peers) + 1
    me = lax.axis_index("cls")
    steps = size // 2
    part = page_ref.shape[0] // 2
    odd = lax.rem(me, 2)
    spot = odd * (size - 1 - me // 2) + (1 - odd) * (me // 2)

    def index_at(position):
        position = lax.rem(position + size, size)
        back = position // steps
        return (1 - back) * 2 * position + back * (2 * (size - 1 - position) + 1)

    nexts = (index_at(spot + 1), index_at(spot - 1))
    greet(peers)
    lists = push(peers, lambda peer: own_ref, inbox, list_sends, list_arrivals)
    local = pltpu.make_async_copy(page_ref, out_ref.at[me], local_sem)
    local.start()
    copies, pending = {}, []
    for step in range(steps):
        for piece in (0, 1):
            for way in (0, 1):
                if step == steps - 1 and way != piece:
                    continue
                rows = pl.ds(piece * part, part)
                owner = index_at(spot - step if way == 0 else spot + step)
                if step:
                    copies[way, step - 1, piece].wait_recv()
                    pending.remove((way, step - 1, piece))
                copy = pltpu.make_async_remote_copy(
                    src_ref=out_ref.at[owner, rows] if step else page_ref.at[rows],
                    dst_ref=out_ref.at[owner, rows],
                    send_sem=sends.at[way, step, piece],
                    recv_sem=arrivals.at[way, step, piece],
                    device_id={"cls": nexts[way]},
                    device_id_type=pl.DeviceIdType.MESH,
                )
                copy.start()
                copies[way, step, piece] = copy
                pending.append((way, step, piece))
    list_ref[me] = own_ref[...]
    for slot, copy in enumerate(lists):
        copy.wait_recv()
        list_ref[lax.rem(me + size - slot - 1, size)] = inbox[slot]
    for key in pending:
        copies[key].wait_recv()
    for copy in lists + list(copies.values()):
        copy.wait_send()
    local.wait()


def reduce_kernel(
    score_ref, out_ref, pair_ref, parts, share, spread, tally, tallies, summed, wide,
    send_a, send_b, send_c, send_d, recv_a, recv_b, recv_c, recv_d,
):
    rots, owners = peers_along("rot"), peers_along("cls")
    splits = len(rots) + 1
    rot = lax.axis_index("rot")
    rows = share.shape[0]
    greet(rots + owners)

    def part(index):
        return pl.ds(pl.multiple_of(index * rows, GROUP), rows)

    first = push(rots, lambda peer: score_ref.at[part(peer["rot"])], parts, send_a, recv_a)
    total = score_ref[part(rot), :]
    for slot, copy in enumerate(first):
        copy.wait_recv()
        total = total + parts[slot]
    share[...] = total
    second = push(rots, lambda peer: share, spread, send_b, recv_b)
    grown = jnp.concatenate(
        [jnp.exp(total), jnp.zeros((tally.shape[1] - rows, LANES), F32)], axis=0
    ).T
    tally[...] = jnp.zeros_like(tally)
    tally[pl.ds(0, 1), :] = jnp.sum(grown[: LANES // 2], axis=0, keepdims=True)
    tally[pl.ds(1, 1), :] = jnp.sum(grown[LANES // 2 :], axis=0, keepdims=True)
    third = push(owners, lambda peer: tally, tallies, send_c, recv_c)
    out_ref[part(rot), :] = total
    sums = tally[...]
    for slot, copy in enumerate(third):
        copy.wait_recv()
        sums = sums + tallies[slot]
    summed[...] = sums
    fourth = push(rots, lambda peer: summed, wide, send_d, recv_d)
    pair_ref[rot] = sums
    for slot in range(len(rots)):
        source = lax.rem(rot + splits - slot - 1, splits)
        second[slot].wait_recv()
        out_ref[part(source), :] = spread[slot]
        fourth[slot].wait_recv()
        pair_ref[source] = wide[slot]
    for copy in first + second + third + fourth:
        copy.wait_send()


def sum_kernel(
    count_ref, list_ref, score_ref, total_ref, image_ref, out_ref, weight, sums, flipped
):
    half = score_ref.shape[0]
    particles = total_ref.shape[0]
    class_local, cycles, angles = out_ref.shape
    lane = lax.broadcasted_iota(jnp.int32, (half, LANES), 1)
    grown = jnp.exp(score_ref[...])
    lows = jnp.where(lane < LANES // 2, grown, 0.0)
    weight[pl.ds(0, half), :] = lows
    weight[pl.ds(half, half), :] = pltpu.roll(grown - lows, LANES // 2, 1)
    inverse = 1.0 / total_ref[...]
    for k in range(2 * half // particles):
        rows = pl.ds(k * particles, particles)
        posterior = weight[rows, :] * inverse
        weight[rows, :] = posterior + pltpu.roll(posterior, LANES - ROTS, 1)
    weight[pl.ds(2 * half, GROUP), :] = jnp.zeros((GROUP, LANES), F32)
    sums[...] = jnp.zeros_like(sums)

    def batch(step, carry):
        products = []
        for member in range(BATCH):
            at = step * BATCH + member
            row = weight[pl.ds(list_ref[0, at], 1), :]
            skewed = pltpu.roll(
                jnp.broadcast_to(row, (ROTS, LANES)), 0, 1, stride=1, stride_axis=0
            )
            image = image_ref[list_ref[1, at]]
            products.append(
                jnp.dot(skewed.astype(BF16)[:, :ROTS], image, preferred_element_type=F32)
            )
        for member in range(BATCH):
            own = list_ref[2, step * BATCH + member]
            sums[own] = sums[own] + products[member]
        return carry

    lax.fori_loop(0, count_ref[0], batch, 0)

    def write(group, carry):
        first = group * GROUP
        pages = swap_blocks([sums[first + member] for member in range(GROUP)])
        for s in range(GROUP):
            flipped[pl.ds(s, ROTS, stride=GROUP), :] = pages[s]
        out_ref[pl.ds(first, GROUP)] = flipped[...].T.reshape(GROUP, SPAN, angles)[:, :cycles]
        return carry

    lax.fori_loop(0, class_local // GROUP, write, 0)


VMEM = pl.BlockSpec(memory_space=pltpu.VMEM)
SMEM = pl.BlockSpec(memory_space=pltpu.SMEM)


def shards(particles, references, noise_weights, offsets, sig_classes):
    owner_count = lax.axis_size("cls")
    split_count = lax.axis_size("rot")
    home_count, cycle_count, angle_count = particles.shape
    class_local = references.shape[0]
    list_length = sig_classes.shape[1]
    particle_count = home_count * owner_count
    cycles = cycle_count // split_count
    pair_count = particle_count * list_length
    half = pair_count // 2
    me = lax.axis_index("cls")
    rot = lax.axis_index("rot").astype(jnp.int32)
    rot_arg = rot.reshape(1)
    limit = pltpu.CompilerParams(vmem_limit_bytes=56 << 20)

    owners, rots = owner_count - 1, split_count - 1
    own_list = jnp.pad(
        sig_classes.T, ((0, GROUP - list_length), (0, LANES - home_count)), constant_values=0
    )
    image_block = (GROUP, cycles, angle_count)
    pages = pl.pallas_call(
        particle_kernel,
        out_shape=jax.ShapeDtypeStruct((home_count, ROTS, LANES), BF16),
        grid_spec=pltpu.PrefetchScalarGridSpec(
            num_scalar_prefetch=2,
            grid=(home_count // GROUP,),
            in_specs=[pl.BlockSpec(image_block, lambda g, r, o: (g, r[0], 0))],
            out_specs=pl.BlockSpec((GROUP, ROTS, LANES), lambda g, r, o: (g, 0, 0)),
            scratch_shapes=[
                pltpu.VMEM((LANES, angle_count), F32),
                pltpu.VMEM((angle_count, LANES), F32),
            ],
        ),
        name="align_particles",
    )(rot_arg, offsets, particles)
    ring = pltpu.SemaphoreType.DMA((2, owner_count // 2, 2))
    gathered, classes = pl.pallas_call(
        gather_kernel,
        out_shape=(
            jax.ShapeDtypeStruct((owner_count,) + pages.shape, BF16),
            jax.ShapeDtypeStruct((owner_count, GROUP, LANES), jnp.int32),
        ),
        in_specs=[VMEM, VMEM],
        out_specs=(pl.BlockSpec(memory_space=pl.ANY), VMEM),
        scratch_shapes=[
            pltpu.VMEM((owners, GROUP, LANES), jnp.int32),
            pltpu.SemaphoreType.DMA,
            pltpu.SemaphoreType.DMA((owners,)),
            pltpu.SemaphoreType.DMA((owners,)),
            ring,
            ring,
        ],
        compiler_params=pltpu.CompilerParams(
            collective_id=1, has_side_effects=True, vmem_limit_bytes=56 << 20
        ),
        name="gather_particles",
    )(pages, own_list)
    gathered = gathered.reshape(particle_count, ROTS, LANES)
    classes = classes[:, :list_length, :home_count].transpose(1, 0, 2).reshape(pair_count)
    pair_iota = jnp.arange(pair_count, dtype=jnp.int32)
    mine = (classes // class_local) == me
    before = pair_iota[None, :] < pair_iota[:, None]
    place = jnp.sum(jnp.where(before & mine[None, :], 1, 0), axis=1)
    count = jnp.sum(mine.astype(jnp.int32))
    slots = jnp.arange(pair_count + BATCH, dtype=jnp.int32)
    hit = (place[None, :] == slots[:, None]) & mine[None, :]
    pick = lambda values: jnp.sum(jnp.where(hit, values[None, :], 0), axis=1)
    unused = jnp.where(slots < count, 0, pair_count)
    work = jnp.stack(
        [
            pick(pair_iota) + unused,
            pick(pair_iota % particle_count),
            pick(classes % class_local),
        ]
    )
    batches = ((count + BATCH - 1) // BATCH).reshape(1)

    own_weights = lax.dynamic_slice_in_dim(noise_weights, rot * cycles, cycles).reshape(cycles, 1)
    class_pages, energy = pl.pallas_call(
        reference_kernel,
        out_shape=(
            jax.ShapeDtypeStruct((class_local, LANES, LANES), BF16),
            jax.ShapeDtypeStruct((class_local, LANES), F32),
        ),
        grid_spec=pltpu.PrefetchScalarGridSpec(
            num_scalar_prefetch=1,
            grid=(class_local // GROUP,),
            in_specs=[
                pl.BlockSpec(image_block, lambda g, r: (g, r[0], 0)),
                pl.BlockSpec((cycles, 1), lambda g, r: (0, 0)),
            ],
            out_specs=(
                pl.BlockSpec((GROUP, LANES, LANES), lambda g, r: (g, 0, 0)),
                pl.BlockSpec((GROUP, LANES), lambda g, r: (g, 0)),
            ),
            scratch_shapes=[pltpu.VMEM((angle_count, LANES), F32)],
        ),
        name="weight_references",
    )(rot_arg, references, own_weights)

    scores = pl.pallas_call(
        score_kernel,
        out_shape=jax.ShapeDtypeStruct((half, LANES), F32),
        in_specs=[SMEM, SMEM, VMEM, VMEM, VMEM],
        out_specs=VMEM,
        scratch_shapes=[pltpu.VMEM((pair_count + GROUP, LANES), F32)],
        compiler_params=limit,
        name="score_pairs",
    )(batches, work, gathered, class_pages, energy)
    share = half // split_count
    wide = -(-share // LANES) * LANES
    tile = pltpu.VMEM((GROUP, wide), F32)
    scores, pair_sums = pl.pallas_call(
        reduce_kernel,
        out_shape=(
            jax.ShapeDtypeStruct((half, LANES), F32),
            jax.ShapeDtypeStruct((split_count, GROUP, wide), F32),
        ),
        in_specs=[VMEM],
        out_specs=(VMEM, VMEM),
        scratch_shapes=[
            pltpu.VMEM((rots, share, LANES), F32),
            pltpu.VMEM((share, LANES), F32),
            pltpu.VMEM((rots, share, LANES), F32),
            tile,
            pltpu.VMEM((owners, GROUP, wide), F32),
            tile,
            pltpu.VMEM((rots, GROUP, wide), F32),
        ]
        + [pltpu.SemaphoreType.DMA((count_of,)) for count_of in (rots, rots, owners, rots)] * 2,
        compiler_params=pltpu.CompilerParams(
            collective_id=2, has_side_effects=True, vmem_limit_bytes=56 << 20
        ),
        name="exchange_scores",
    )(scores)
    pair_sums = pair_sums[:, :2, :share].transpose(1, 0, 2).reshape(list_length, particle_count)
    total = jnp.sum(pair_sums, axis=0)

    class_sums = pl.pallas_call(
        sum_kernel,
        out_shape=jax.ShapeDtypeStruct((class_local, cycles, angle_count), F32),
        in_specs=[SMEM, SMEM, VMEM, VMEM, VMEM],
        out_specs=VMEM,
        scratch_shapes=[
            pltpu.VMEM((pair_count + GROUP, LANES), F32),
            pltpu.VMEM((class_local, ROTS, LANES), F32),
            pltpu.VMEM((angle_count, LANES), F32),
        ],
        compiler_params=limit,
        name="sum_classes",
    )(batches, work, scores, total.reshape(particle_count, 1), gathered)
    own_total = lax.dynamic_slice_in_dim(total, me * home_count, home_count)
    return (jnp.log(own_total), class_sums)


def solution(mesh):
    in_specs = (P("cls", None, None), P("cls", None, None), P(), P("cls"), P("cls", None))
    out_specs = (P("cls"), P("cls", "rot", None))
    return jax.shard_map(shards, mesh=mesh, in_specs=in_specs, out_specs=out_specs, check_vma=False)
```

```python
import functools

import jax
import jax.numpy as jnp
from jax import lax
from jax.experimental import pallas as pl
from jax.experimental.pallas import tpu as pltpu
from jax.sharding import PartitionSpec as P

ROTS = 48
GROUP = 8
LANES = 128
SPAN = LANES // GROUP
BATCH = 8
UNLISTED = -1e30
F32 = jnp.float32
BF16 = jnp.bfloat16


def swap_blocks(pages):
    block = lax.broadcasted_iota(jnp.int32, pages[0].shape, 1) // SPAN
    for step in (1, 2, 4):
        high = (block & step) != 0
        changed = list(pages)
        for low_index in range(GROUP):
            if low_index & step:
                continue
            low_page, high_page = pages[low_index], pages[low_index | step]
            changed[low_index] = jnp.where(high, pltpu.roll(high_page, SPAN * step, 1), low_page)
            changed[low_index | step] = jnp.where(
                high, high_page, pltpu.roll(low_page, LANES - SPAN * step, 1)
            )
        pages = changed
    return pages


def split_angles(rows, flipped):
    flipped[...] = rows.T
    return swap_blocks([flipped[pl.ds(s, ROTS, stride=GROUP), :] for s in range(GROUP)])


def particle_kernel(rot_ref, offset_ref, image_ref, page_ref, rows, flipped):
    first = pl.program_id(0) * GROUP
    cycles, angles = image_ref.shape[1:]
    if cycles < SPAN:
        rows[...] = jnp.zeros_like(rows)
    for member in range(GROUP):
        shift = lax.rem(angles - offset_ref[first + member], angles)
        rows[pl.ds(member * SPAN, cycles), :] = pltpu.roll(
            image_ref[member].astype(F32), shift, 1
        )
    pages = split_angles(rows[...], flipped)
    for member in range(GROUP):
        page_ref[member] = pages[member].astype(BF16)


def reference_kernel(rot_ref, image_ref, weight_ref, page_ref, energy_ref, flipped):
    cycles, angles = image_ref.shape[1:]
    images = image_ref[...].astype(F32)
    weights = weight_ref[...][None]
    weighted = (images * weights).astype(BF16).astype(F32)
    energy = jnp.sum(jnp.sum(weights * images * images, axis=2), axis=1, keepdims=True)
    energy_ref[...] = jnp.broadcast_to(0.5 * energy, energy_ref.shape)
    if cycles < SPAN:
        spare = jnp.zeros((GROUP, SPAN - cycles, angles), F32)
        weighted = jnp.concatenate([weighted, spare], axis=1)
    pages = split_angles(weighted.reshape(LANES, angles), flipped)
    source = lax.broadcasted_iota(jnp.int32, (ROTS, LANES), 0)
    target = lax.broadcasted_iota(jnp.int32, (ROTS, LANES), 1)
    reverse = jnp.where(lax.rem(source + target, ROTS) == 0, 1.0, 0.0).astype(BF16)
    for member in range(GROUP):
        page_ref[member] = lax.dot_general(
            pages[member].astype(BF16), reverse, (((0,), (0,)), ((), ())), preferred_element_type=F32
        ).astype(BF16)


def score_kernel(count_ref, list_ref, image_ref, class_ref, energy_ref, out_ref, held):
    held[...] = jnp.full_like(held, UNLISTED)
    half = out_ref.shape[0]

    def batch(step, carry):
        products = []
        for member in range(BATCH):
            at = step * BATCH + member
            image = image_ref[list_ref[1, at]]
            products.append(
                jnp.dot(image, class_ref[list_ref[2, at]], preferred_element_type=F32)
            )
        for member in range(BATCH):
            at = step * BATCH + member
            skewed = pltpu.roll(products[member], 0, 1, stride=1, stride_axis=0)
            score = jnp.sum(skewed, axis=0, keepdims=True)
            held[pl.ds(list_ref[0, at], 1), :] = score - energy_ref[pl.ds(list_ref[2, at], 1), :]
        return carry

    lax.fori_loop(0, count_ref[0], batch, 0)
    lane = lax.broadcasted_iota(jnp.int32, (half, LANES), 1)
    low = pltpu.roll(held[pl.ds(0, half), :], LANES - ROTS, 1)
    high = pltpu.roll(held[pl.ds(half, half), :], LANES // 2 - ROTS, 1)
    inside = (lane % (LANES // 2)) < ROTS
    out_ref[...] = jnp.where(inside, jnp.where(lane < LANES // 2, low, high), UNLISTED)


def push(peers, source, inbox, sends, arrivals):
    copies = [
        pltpu.make_async_remote_copy(
            src_ref=source(peer),
            dst_ref=inbox.at[slot],
            send_sem=sends.at[slot],
            recv_sem=arrivals.at[slot],
            device_id=peer,
            device_id_type=pl.DeviceIdType.MESH,
        )
        for slot, peer in enumerate(peers)
    ]
    for copy in copies:
        copy.start()
    return copies


def peers_along(axis):
    size = lax.axis_size(axis)
    own = lax.axis_index(axis)
    return [{axis: lax.rem(own + step, size)} for step in range(1, size)]


def greet(peers):
    barrier = pltpu.get_barrier_semaphore()
    for peer in peers:
        pl.semaphore_signal(barrier, inc=1, device_id=peer, device_id_type=pl.DeviceIdType.MESH)
    pl.semaphore_wait(barrier, len(peers))


def gather_kernel(
    page_ref, own_ref, image_ref, weight_ref, out_ref, list_ref, class_ref, energy_ref,
    inbox, images, flipped, image_sem, local_sem, list_sends, list_arrivals, sends, arrivals,
):
    peers = peers_along("cls")
    size = len(peers) + 1
    me = lax.axis_index("cls")
    steps = size // 2
    part = page_ref.shape[0] // 2
    odd = lax.rem(me, 2)
    spot = odd * (size - 1 - me // 2) + (1 - odd) * (me // 2)

    def index_at(position):
        position = lax.rem(position + size, size)
        back = position // steps
        return (1 - back) * 2 * position + back * (2 * (size - 1 - position) + 1)

    nexts = (index_at(spot + 1), index_at(spot - 1))
    cycles = images.shape[1]
    first = pl.multiple_of(lax.axis_index("rot") * cycles, cycles)
    fetch = pltpu.make_async_copy(image_ref.at[:, pl.ds(first, cycles), :], images, image_sem)
    fetch.start()

    def weigh(group, carry):
        rows = pl.ds(group * GROUP, GROUP)
        reference_kernel(
            None, images.at[rows], weight_ref, class_ref.at[rows], energy_ref.at[rows], flipped
        )
        return carry

    greet(peers)
    lists = push(peers, lambda peer: own_ref, inbox, list_sends, list_arrivals)
    local = pltpu.make_async_copy(page_ref, out_ref.at[me], local_sem)
    local.start()
    copies, pending = {}, []
    for step in range(steps):
        for piece in (0, 1):
            for way in (0, 1):
                if step == steps - 1 and way != piece:
                    continue
                rows = pl.ds(piece * part, part)
                owner = index_at(spot - step if way == 0 else spot + step)
                if step:
                    copies[way, step - 1, piece].wait_recv()
                    pending.remove((way, step - 1, piece))
                copy = pltpu.make_async_remote_copy(
                    src_ref=out_ref.at[owner, rows] if step else page_ref.at[rows],
                    dst_ref=out_ref.at[owner, rows],
                    send_sem=sends.at[way, step, piece],
                    recv_sem=arrivals.at[way, step, piece],
                    device_id={"cls": nexts[way]},
                    device_id_type=pl.DeviceIdType.MESH,
                )
                copy.start()
                copies[way, step, piece] = copy
                pending.append((way, step, piece))
        if step == 0:
            fetch.wait()
            lax.fori_loop(0, images.shape[0] // GROUP, weigh, 0)
    list_ref[me] = own_ref[...]
    for slot, copy in enumerate(lists):
        copy.wait_recv()
        list_ref[lax.rem(me + size - slot - 1, size)] = inbox[slot]
    for key in pending:
        copies[key].wait_recv()
    for copy in lists + list(copies.values()):
        copy.wait_send()
    local.wait()


def reduce_kernel(
    score_ref, out_ref, pair_ref, parts, share, spread, tally, tallies, summed, wide,
    send_a, send_b, send_c, send_d, recv_a, recv_b, recv_c, recv_d,
):
    rots, owners = peers_along("rot"), peers_along("cls")
    splits = len(rots) + 1
    rot = lax.axis_index("rot")
    rows = share.shape[0]
    greet(rots + owners)

    def part(index):
        return pl.ds(pl.multiple_of(index * rows, GROUP), rows)

    first = push(rots, lambda peer: score_ref.at[part(peer["rot"])], parts, send_a, recv_a)
    total = score_ref[part(rot), :]
    for slot, copy in enumerate(first):
        copy.wait_recv()
        total = total + parts[slot]
    share[...] = total
    second = push(rots, lambda peer: share, spread, send_b, recv_b)
    grown = jnp.concatenate(
        [jnp.exp(total), jnp.zeros((tally.shape[1] - rows, LANES), F32)], axis=0
    ).T
    tally[...] = jnp.zeros_like(tally)
    tally[pl.ds(0, 1), :] = jnp.sum(grown[: LANES // 2], axis=0, keepdims=True)
    tally[pl.ds(1, 1), :] = jnp.sum(grown[LANES // 2 :], axis=0, keepdims=True)
    third = push(owners, lambda peer: tally, tallies, send_c, recv_c)
    out_ref[part(rot), :] = total
    sums = tally[...]
    for slot, copy in enumerate(third):
        copy.wait_recv()
        sums = sums + tallies[slot]
    summed[...] = sums
    fourth = push(rots, lambda peer: summed, wide, send_d, recv_d)
    pair_ref[rot] = sums
    for slot in range(len(rots)):
        source = lax.rem(rot + splits - slot - 1, splits)
        second[slot].wait_recv()
        out_ref[part(source), :] = spread[slot]
        fourth[slot].wait_recv()
        pair_ref[source] = wide[slot]
    for copy in first + second + third + fourth:
        copy.wait_send()


def sum_kernel(
    count_ref, list_ref, score_ref, total_ref, image_ref, out_ref, weight, sums, flipped
):
    half = score_ref.shape[0]
    particles = total_ref.shape[0]
    class_local, cycles, angles = out_ref.shape
    lane = lax.broadcasted_iota(jnp.int32, (half, LANES), 1)
    grown = jnp.exp(score_ref[...])
    lows = jnp.where(lane < LANES // 2, grown, 0.0)
    weight[pl.ds(0, half), :] = lows
    weight[pl.ds(half, half), :] = pltpu.roll(grown - lows, LANES // 2, 1)
    inverse = 1.0 / total_ref[...]
    for k in range(2 * half // particles):
        rows = pl.ds(k * particles, particles)
        posterior = weight[rows, :] * inverse
        weight[rows, :] = posterior + pltpu.roll(posterior, LANES - ROTS, 1)
    weight[pl.ds(2 * half, GROUP), :] = jnp.zeros((GROUP, LANES), F32)
    sums[...] = jnp.zeros_like(sums)

    def batch(step, carry):
        products = []
        for member in range(BATCH):
            at = step * BATCH + member
            row = weight[pl.ds(list_ref[0, at], 1), :]
            skewed = pltpu.roll(
                jnp.broadcast_to(row, (ROTS, LANES)), 0, 1, stride=1, stride_axis=0
            )
            image = image_ref[list_ref[1, at]]
            products.append(
                jnp.dot(skewed.astype(BF16)[:, :ROTS], image, preferred_element_type=F32)
            )
        for member in range(BATCH):
            own = list_ref[2, step * BATCH + member]
            sums[own] = sums[own] + products[member]
        return carry

    lax.fori_loop(0, count_ref[0], batch, 0)

    def write(group, carry):
        first = group * GROUP
        pages = swap_blocks([sums[first + member] for member in range(GROUP)])
        for s in range(GROUP):
            flipped[pl.ds(s, ROTS, stride=GROUP), :] = pages[s]
        out_ref[pl.ds(first, GROUP)] = flipped[...].T.reshape(GROUP, SPAN, angles)[:, :cycles]
        return carry

    lax.fori_loop(0, class_local // GROUP, write, 0)


VMEM = pl.BlockSpec(memory_space=pltpu.VMEM)
SMEM = pl.BlockSpec(memory_space=pltpu.SMEM)


def shards(particles, references, noise_weights, offsets, sig_classes):
    owner_count = lax.axis_size("cls")
    split_count = lax.axis_size("rot")
    home_count, cycle_count, angle_count = particles.shape
    class_local = references.shape[0]
    list_length = sig_classes.shape[1]
    particle_count = home_count * owner_count
    cycles = cycle_count // split_count
    pair_count = particle_count * list_length
    half = pair_count // 2
    me = lax.axis_index("cls")
    rot = lax.axis_index("rot").astype(jnp.int32)
    rot_arg = rot.reshape(1)
    limit = pltpu.CompilerParams(vmem_limit_bytes=56 << 20)

    owners, rots = owner_count - 1, split_count - 1
    own_list = jnp.pad(
        sig_classes.T, ((0, GROUP - list_length), (0, LANES - home_count)), constant_values=0
    )
    image_block = (GROUP, cycles, angle_count)
    pages = pl.pallas_call(
        particle_kernel,
        out_shape=jax.ShapeDtypeStruct((home_count, ROTS, LANES), BF16),
        grid_spec=pltpu.PrefetchScalarGridSpec(
            num_scalar_prefetch=2,
            grid=(home_count // GROUP,),
            in_specs=[pl.BlockSpec(image_block, lambda g, r, o: (g, r[0], 0))],
            out_specs=pl.BlockSpec((GROUP, ROTS, LANES), lambda g, r, o: (g, 0, 0)),
            scratch_shapes=[
                pltpu.VMEM((LANES, angle_count), F32),
                pltpu.VMEM((angle_count, LANES), F32),
            ],
        ),
        name="align_particles",
    )(rot_arg, offsets, particles)
    own_weights = lax.dynamic_slice_in_dim(noise_weights, rot * cycles, cycles).reshape(cycles, 1)
    ring = pltpu.SemaphoreType.DMA((2, owner_count // 2, 2))
    gathered, classes, class_pages, energy = pl.pallas_call(
        gather_kernel,
        out_shape=(
            jax.ShapeDtypeStruct((owner_count,) + pages.shape, BF16),
            jax.ShapeDtypeStruct((owner_count, GROUP, LANES), jnp.int32),
            jax.ShapeDtypeStruct((class_local, LANES, LANES), BF16),
            jax.ShapeDtypeStruct((class_local, LANES), F32),
        ),
        in_specs=[VMEM, VMEM, pl.BlockSpec(memory_space=pl.ANY), VMEM],
        out_specs=(pl.BlockSpec(memory_space=pl.ANY), VMEM, VMEM, VMEM),
        scratch_shapes=[
            pltpu.VMEM((owners, GROUP, LANES), jnp.int32),
            pltpu.VMEM((class_local, cycles, angle_count), BF16),
            pltpu.VMEM((angle_count, LANES), F32),
            pltpu.SemaphoreType.DMA,
            pltpu.SemaphoreType.DMA,
            pltpu.SemaphoreType.DMA((owners,)),
            pltpu.SemaphoreType.DMA((owners,)),
            ring,
            ring,
        ],
        compiler_params=pltpu.CompilerParams(
            collective_id=1, has_side_effects=True, vmem_limit_bytes=56 << 20
        ),
        name="gather_particles",
    )(pages, own_list, references, own_weights)
    gathered = gathered.reshape(particle_count, ROTS, LANES)
    classes = classes[:, :list_length, :home_count].transpose(1, 0, 2).reshape(pair_count)
    pair_iota = jnp.arange(pair_count, dtype=jnp.int32)
    mine = (classes // class_local) == me
    before = pair_iota[None, :] < pair_iota[:, None]
    place = jnp.sum(jnp.where(before & mine[None, :], 1, 0), axis=1)
    count = jnp.sum(mine.astype(jnp.int32))
    slots = jnp.arange(pair_count + BATCH, dtype=jnp.int32)
    hit = (place[None, :] == slots[:, None]) & mine[None, :]
    pick = lambda values: jnp.sum(jnp.where(hit, values[None, :], 0), axis=1)
    unused = jnp.where(slots < count, 0, pair_count)
    work = jnp.stack(
        [
            pick(pair_iota) + unused,
            pick(pair_iota % particle_count),
            pick(classes % class_local),
        ]
    )
    batches = ((count + BATCH - 1) // BATCH).reshape(1)

    scores = pl.pallas_call(
        score_kernel,
        out_shape=jax.ShapeDtypeStruct((half, LANES), F32),
        in_specs=[SMEM, SMEM, VMEM, VMEM, VMEM],
        out_specs=VMEM,
        scratch_shapes=[pltpu.VMEM((pair_count + GROUP, LANES), F32)],
        compiler_params=limit,
        name="score_pairs",
    )(batches, work, gathered, class_pages, energy)
    share = half // split_count
    wide = -(-share // LANES) * LANES
    tile = pltpu.VMEM((GROUP, wide), F32)
    scores, pair_sums = pl.pallas_call(
        reduce_kernel,
        out_shape=(
            jax.ShapeDtypeStruct((half, LANES), F32),
            jax.ShapeDtypeStruct((split_count, GROUP, wide), F32),
        ),
        in_specs=[VMEM],
        out_specs=(VMEM, VMEM),
        scratch_shapes=[
            pltpu.VMEM((rots, share, LANES), F32),
            pltpu.VMEM((share, LANES), F32),
            pltpu.VMEM((rots, share, LANES), F32),
            tile,
            pltpu.VMEM((owners, GROUP, wide), F32),
            tile,
            pltpu.VMEM((rots, GROUP, wide), F32),
        ]
        + [pltpu.SemaphoreType.DMA((count_of,)) for count_of in (rots, rots, owners, rots)] * 2,
        compiler_params=pltpu.CompilerParams(
            collective_id=2, has_side_effects=True, vmem_limit_bytes=56 << 20
        ),
        name="exchange_scores",
    )(scores)
    pair_sums = pair_sums[:, :2, :share].transpose(1, 0, 2).reshape(list_length, particle_count)
    total = jnp.sum(pair_sums, axis=0)

    class_sums = pl.pallas_call(
        sum_kernel,
        out_shape=jax.ShapeDtypeStruct((class_local, cycles, angle_count), F32),
        in_specs=[SMEM, SMEM, VMEM, VMEM, VMEM],
        out_specs=VMEM,
        scratch_shapes=[
            pltpu.VMEM((pair_count + GROUP, LANES), F32),
            pltpu.VMEM((class_local, ROTS, LANES), F32),
            pltpu.VMEM((angle_count, LANES), F32),
        ],
        compiler_params=limit,
        name="sum_classes",
    )(batches, work, scores, total.reshape(particle_count, 1), gathered)
    own_total = lax.dynamic_slice_in_dim(total, me * home_count, home_count)
    return (jnp.log(own_total), class_sums)


def solution(mesh):
    in_specs = (P("cls", None, None), P("cls", None, None), P(), P("cls"), P("cls", None))
    out_specs = (P("cls"), P("cls", "rot", None))
    return jax.shard_map(shards, mesh=mesh, in_specs=in_specs, out_specs=out_specs, check_vma=False)
```
